256 devices in a mesh: ep: 64 (over z, x, core), rep: 4 (over y).
Axes of the slice: x: 4, y: 4, z: 8, core: 2. Of those that a mesh axis runs over, the one named last changes fastest.
Arguments:
- tokens_one: bfloat16 [2048, 7168], P('ep', 'rep'), may hold values from -6 to 6
- tokens_two: bfloat16 [2048, 7168], P('ep', 'rep'), may hold values from -6 to 6
- routes_one: int32 [2048, 8], P('ep'), may hold values from 0 to 63, all different within a row; in each aligned block of 32 rows (0 to 31, 32 to 63, ...) at most 8 rows name the same one
- routes_two: int32 [2048, 8], P('ep'), may hold values from 0 to 63, all different within a row; in each aligned block of 32 rows (0 to 31, 32 to 63, ...) at most 8 rows name the same one
- gates_one: float32 [2048, 8], P('ep'), may hold values from 0.1 to 0.6
- gates_two: float32 [2048, 8], P('ep'), may hold values from 0.1 to 0.6
- place_before: int32 [64], replicated, may hold values from 0 to 63, each once
- swap_flags: int32 [32], replicated, may hold values 0 or 1
- gate_weight: bfloat16 [64, 7168, 1024], P('ep', 'rep'), may hold values from -0.0625 to 0.0625
- up_weight: bfloat16 [64, 7168, 1024], P('ep', 'rep'), may hold values from -0.0625 to 0.0625
- down_weight: bfloat16 [64, 1024, 7168], P('ep', None, 'rep'), may hold values from -0.1875 to 0.1875
Outputs:
- mixed_one: bfloat16 [2048, 7168], P('ep', 'rep')
- mixed_two: bfloat16 [2048, 7168], P('ep', 'rep')
The draws below stay inside these ranges and needn't reach their ends.
Inputs may be any that keep to these rules, and one draw needn't show every extreme that they name: `routes_one`: in each aligned block of 32 rows (the rows of one index of ep) no expert is named more than 8 times, and in every draw some expert is named exactly 8 times in some block; a row names 8 different experts. `routes_two`: in each aligned block of 32 rows (the rows of one index of ep) no ep index is named more than 8 times, and in every draw some is named exactly 8 times in some block; a row names 8 different ep indices. `place_before`: each ep index appears once.
All inputs are finite; a program needn't handle non-finite values.
Results may differ from the reference program's by a relative error of at most 0.0058.
Values may be sent and summed in bfloat16 or wider, within the bound.
A program may use at most 128 MiB of HBM per device.

```python
import math
import jax
import jax.numpy as jnp
import numpy as np
from jax import lax

D = 7168
FH = 1024
TOP = 8
R_EP = 32
MOST = 8
EXPERTS = 64
HALF = 32
TOKENS = 2048
N_EP = 64


def place_ends(result, rng, least, largest):
    place = [jax.random.randint(jax.random.fold_in(rng, axis), (), 0, length) for axis, length in enumerate(result.shape)]
    longest = result.shape.index(max(result.shape))
    beside = place[:longest] + [(place[longest] + 1) % result.shape[longest]] + place[longest + 1:]
    return result.at[tuple(place)].set(least).at[tuple(beside)].set(largest)


def level_of(stream_key, shape, shards, least, high):
    gain = 1.0
    for position, blocks in shards:
        heights = jax.random.uniform(jax.random.fold_in(jax.random.fold_in(stream_key, 6), position), (blocks,), jnp.float32, least / len(shards), high / len(shards))
        gain = gain * jnp.repeat(jnp.exp(heights), shape[position] // blocks).reshape((-1,) + (1,) * (len(shape) - 1 - position))
    return gain


def deal_out(rng, own, number, rows, count, top, reach, slope):
    sequence = jax.random.permutation(rng, count)
    packed, usual = load_shares(count, rows * top, reach, slope, True), load_shares(count, rows * top, reach, slope, False)
    places = jnp.arange(count)

    def named(tallies, rotation):
        used = int((tallies > 0).sum())
        fixed = max(1, used // 4)
        shifted = fixed + (places - fixed + rotation * (used - fixed)) % max(1, count - fixed)
        return jnp.zeros((count,), jnp.int32).at[sequence[jnp.where(places < fixed, places, shifted)]].set(jnp.asarray(tallies, jnp.int32))

    tallies = jnp.where(number % 4 == 0, named(packed, number // 4), named(usual, number - number // 4 - 1))
    mixed = jax.random.permutation(jax.random.fold_in(own, 3), count)
    giver, receiver = mixed[0:count // 2 * 2:2], mixed[1:count // 2 * 2:2]
    margin = jnp.minimum(tallies[giver] - 1, reach - tallies[receiver]) // 2
    margin = jnp.where((giver == sequence[0]) | (receiver == sequence[0]) | (tallies[receiver] == 0), 0, jnp.maximum(margin, 0))
    shifted = jax.random.randint(jax.random.fold_in(own, 4), (count // 2,), 0, 1 << 20) % (margin + 1)
    tallies = tallies.at[giver].add(-shifted).at[receiver].add(shifted)
    labels = jnp.searchsorted(jnp.cumsum(tallies), jnp.arange(rows * top), side="right").astype(jnp.int32)
    listing = labels.reshape(top, rows).T
    listing = listing[jax.random.permutation(jax.random.fold_in(own, 1), rows)]
    rotation = jax.random.randint(jax.random.fold_in(own, 2), (rows, 1), 0, top)
    return jnp.take_along_axis(listing, (jnp.arange(top)[None, :] + rotation) % top, axis=1)


def load_shares(count, total, most, lean, full):
    loads = [(1 << 20) // math.isqrt(rank ** lean) + 1 for rank in range(1, count + 1)]
    largest = most if full else min(most, max(-(-total // count), total * loads[0] // sum(loads)))
    least = 1 if total - largest >= count - 1 else 0
    counts, spare = [largest] + [least] * (count - 1), total - largest - least * (count - 1)
    while spare > 0:
        movable = [i for i in range(1, count) if counts[i] < largest] or [i for i in range(1, count) if counts[i] < most]
        pool, left = sum([loads[i] for i in movable]), spare
        for i in movable:
            extra = min(most - counts[i], max(1, left * loads[i] // pool), spare)
            counts[i] = counts[i] + extra
            spare = spare - extra
    return np.array(counts)


def centred(rng, shape, scale, bound, shards=(), held_as=jnp.bfloat16):
    gain = level_of(rng, shape, shards, -0.22, 0.18) if shards else 1.0
    entries = jax.random.normal(rng, shape, jnp.float32) * scale * gain
    return jnp.minimum(jnp.maximum(entries, -bound), bound).astype(held_as)


def setup_inputs(seed: int = 0) -> dict:
    arg_keys = jax.random.split(jax.random.key(seed), 12)
    tokens_one = centred(arg_keys[0], (TOKENS, D), 1.0, 6.0, ((0, 64), (1, 4)))
    tokens_two = centred(arg_keys[1], (TOKENS, D), 1.0, 6.0, ((0, 64), (1, 4)))
    routes_one_keys = jax.random.split(jax.random.fold_in(arg_keys[2], 1), TOKENS // R_EP)
    routes_one_turns = jax.random.permutation(jax.random.fold_in(arg_keys[2], 3), TOKENS // R_EP)
    routes_one = jax.vmap(lambda own, number: deal_out(jax.random.fold_in(arg_keys[2], 2), own, number, R_EP, N_EP, TOP, MOST, 2))(routes_one_keys, routes_one_turns).reshape((TOKENS, TOP))
    routes_two_keys = jax.random.split(jax.random.fold_in(arg_keys[3], 1), TOKENS // R_EP)
    routes_two_turns = jax.random.permutation(jax.random.fold_in(arg_keys[3], 3), TOKENS // R_EP)
    routes_two = jax.vmap(lambda own, number: deal_out(jax.random.fold_in(arg_keys[3], 2), own, number, R_EP, N_EP, TOP, MOST, 2))(routes_two_keys, routes_two_turns).reshape((TOKENS, TOP))
    gates_one = jnp.clip(0.1 + 0.5 * jax.random.uniform(arg_keys[4], (TOKENS, TOP), jnp.float32) ** level_of(arg_keys[4], (TOKENS, TOP), ((0, 64),), -0.2, 0.2), 0.1, 0.6)
    gates_two = jnp.clip(0.1 + 0.5 * jax.random.uniform(arg_keys[5], (TOKENS, TOP), jnp.float32) ** level_of(arg_keys[5], (TOKENS, TOP), ((0, 64),), -0.2, 0.2), 0.1, 0.6)
    place_before = jax.random.permutation(arg_keys[6], N_EP).astype(jnp.int32)
    swap_flags = place_ends((jax.random.randint(arg_keys[7], (HALF,), 0, 2) < 1).astype(jnp.int32), jax.random.fold_in(arg_keys[7], 1), 0, 1)
    gate_weight = centred(arg_keys[8], (EXPERTS, D, FH), D ** -0.5, 0.0625, ((0, 64), (1, 4)))
    up_weight = centred(arg_keys[9], (EXPERTS, D, FH), D ** -0.5, 0.0625, ((0, 64), (1, 4)))
    down_weight = centred(arg_keys[10], (EXPERTS, FH, D), FH ** -0.5, 0.1875, ((0, 64), (2, 4)))
    return dict(tokens_one=tokens_one, tokens_two=tokens_two, routes_one=routes_one, routes_two=routes_two, gates_one=gates_one, gates_two=gates_two, place_before=place_before, swap_flags=swap_flags, gate_weight=gate_weight, up_weight=up_weight, down_weight=down_weight)


def expert_rows(row_block, gate_mat, up_mat, down_mat):
    gate_val = jnp.dot(row_block, gate_mat, preferred_element_type=jnp.float32)
    up_val = jnp.dot(row_block, up_mat, preferred_element_type=jnp.float32)
    hidden = (jax.nn.silu(gate_val) * up_val).astype(jnp.bfloat16)
    return jnp.dot(hidden, down_mat, preferred_element_type=jnp.float32).astype(jnp.bfloat16)


def mixture(tokens, slots, gates, gate_weight, up_weight, down_weight, source_slot):
    capacity = N_EP * MOST

    def add_slot(running, slot_id):
        is_named = slots == slot_id
        is_used = jnp.any(is_named, axis=1)
        row_index = jnp.nonzero(is_used, size=capacity, fill_value=0)[0].astype(jnp.int32)
        is_valid = jnp.arange(capacity) < jnp.sum(is_used.astype(jnp.int32))
        holder = source_slot[slot_id]
        expert_out = expert_rows(tokens[row_index], gate_weight[holder], up_weight[holder], down_weight[holder])
        weight = jnp.sum(jnp.where(is_named[row_index], gates[row_index], 0.0), axis=1)
        weight = jnp.where(is_valid, weight, 0.0)
        running = running.at[row_index].add(weight[:, None] * expert_out.astype(jnp.float32))
        return running, None

    initial = jnp.zeros((tokens.shape[0], tokens.shape[1]), jnp.float32)
    running, unused = lax.scan(add_slot, initial, jnp.arange(EXPERTS, dtype=jnp.int32))
    return running.astype(jnp.bfloat16)


def reference(tokens_one, tokens_two, routes_one, routes_two, gates_one, gates_two, place_before, swap_flags, gate_weight, up_weight, down_weight):
    indices = jnp.arange(EXPERTS, dtype=jnp.int32)
    slots_one = jnp.take(place_before, routes_one, axis=0)
    mixed_one = mixture(tokens_one, slots_one, gates_one, gate_weight, up_weight, down_weight, indices)
    partner = jnp.where(indices < HALF, indices + HALF, indices - HALF)
    flagged = jnp.take(swap_flags, indices % HALF, axis=0) == 1
    source_two = jnp.where(flagged, partner, indices)
    mixed_two = mixture(tokens_two, routes_two, gates_two, gate_weight, up_weight, down_weight, source_two)
    return mixed_one, mixed_two
```

```python
import functools

import jax
import jax.numpy as jnp
from jax import lax
from jax.experimental import pallas as pl
from jax.experimental.pallas import tpu as pltpu
from jax.sharding import PartitionSpec as P

NEAR = 8
MOST = 8
META = 128
HALVES = 2
FAR_ORDER = (0, 1, 7, 2, 6, 3, 5, 4)
ORDER = (
    "S0", "G0", "S1", "S2", "A0", "G1", "D0", "G2", "S3", "A1", "D1",
    "M0", "G3", "A2", "D2", "M1", "F0", "A3", "D3", "M2", "M3", "F1",
)
MESH = pl.DeviceIdType.MESH


def dot(a, b):
    return jnp.dot(a, b, preferred_element_type=jnp.float32)


def dot_nt(a, b):
    return lax.dot_general(a, b, (((1,), (1,)), ((), ())), preferred_element_type=jnp.float32)


def iota(shape, dim):
    return lax.broadcasted_iota(jnp.int32, shape, dim)


def kernel(
    tok_one, tok_two, wg_hbm, wu_hbm, wd_hbm,
    out_one, out_two,
    held, outgo, incoming, part, own, temp, arrived, hidden, expert_out, returned, w_high, w_low, mixed, gathered, kept,
    wg, wu, wd,
    w_sem, a_s, a_r, b_s, b_r, y_s, y_r, h_s, h_r, c_s, c_r, d_s, d_r,
):
    rows, padded = tok_one.shape
    width = padded - META
    fh = wg.shape[1]
    far = held.shape[1] // rows
    reps = arrived.shape[1] + 1
    waves = outgo.shape[0]
    halves = waves // 2
    src_count = far // halves
    n = src_count * rows
    share = src_count * MOST
    total = NEAR * share
    piece = total // reps
    order = FAR_ORDER if far == 8 else tuple(range(far))

    ep = lax.axis_index("ep")
    y = lax.axis_index("rep")
    z = ep // NEAR
    near = lax.rem(ep, NEAR)

    def near_dev(r):
        return (z * NEAR + lax.rem(near + r, NEAR), y)

    def far_dev(r):
        return (lax.rem(z + r + far, far) * NEAR + near, y)

    def rep_dev(r):
        return (ep, lax.rem(y + r, reps))

    def copy(src, dst, send, recv, device):
        return pltpu.make_async_remote_copy(
            src_ref=src, dst_ref=dst, send_sem=send, recv_sem=recv, device_id=device, device_id_type=MESH
        )

    toks = (tok_one, tok_two)
    outs = (out_one, out_two)
    a, b, yy, hh, c, d = {}, {}, {}, {}, {}, {}

    loads = [pltpu.make_async_copy(src, dst, w_sem.at[i]) for i, (src, dst) in enumerate(((wg_hbm, wg), (wu_hbm, wu), (wd_hbm, wd)))]
    for load in loads:
        load.start()

    barrier = pltpu.get_barrier_semaphore()
    partners = [near_dev(r) for r in range(1, NEAR)] + [far_dev(r) for r in range(1, far)] + [rep_dev(r) for r in range(1, reps)]
    for device in partners:
        pl.semaphore_signal(barrier, inc=1, device_id=device, device_id_type=MESH)
    pl.semaphore_wait(barrier, len(partners))

    for step in range(2):
        for k in range(1, far):
            a[step, k] = copy(
                toks[step], held.at[step, pl.ds(k * rows, rows)], a_s.at[step, k - 1], a_r.at[step, k - 1], far_dev(order[k])
            )
            a[step, k].start()
    for step in range(2):
        held[step, 0:rows, :] = toks[step][...]

    def select(w):
        step, half = divmod(w, halves)
        for k in range(half * src_count, (half + 1) * src_count):
            if k:
                a[step, k].wait_recv()
        base = half * n
        meta = held[step, base : base + n, width:padded]
        row_expert = z * NEAR + lax.rem(near + iota((total, META), 0) // share, NEAR)
        pick = jnp.where(iota((total, META), 1) == row_expert, 1.0, 0.0).astype(jnp.bfloat16)
        value = dot_nt(pick, meta)
        same = iota((n, n), 0) // rows == iota((n, n), 1) // rows
        upto = jnp.where(same & (iota((n, n), 0) <= iota((n, n), 1)), 1.0, 0.0).astype(jnp.bfloat16)
        count = dot(jnp.where(value > 0.0, 1.0, 0.0).astype(jnp.bfloat16), upto)
        place = lax.rem(iota((total, n), 0), MOST)
        source = lax.rem(iota((total, n), 0), share) // MOST
        good = (value > 0.0) & (count == (place + 1).astype(jnp.float32)) & (iota((total, n), 1) // rows == source)
        chosen = jnp.where(good, 1.0, 0.0).astype(jnp.bfloat16)
        tile = 256 if width % 256 == 0 else 128

        @pl.loop(0, width // tile)
        def _(j):
            cols = pl.ds(pl.multiple_of(j * tile, tile), tile)
            out = dot(chosen, held[step, base : base + n, cols]).astype(jnp.bfloat16)
            outgo[w, :, cols] = out
            incoming[w, 0:share, cols] = out[0:share]

        for r in range(1, NEAR):
            span = pl.ds(r * share, share)
            b[w, r] = copy(outgo.at[w, span], incoming.at[w, span], b_s.at[w, r - 1], b_r.at[w, r - 1], near_dev(r))
            b[w, r].start()

        col_expert = z * NEAR + lax.rem(near + iota((META, total), 1) // share, NEAR)
        high = jnp.where(iota((META, total), 0) == col_expert, 1.0, 0.0).astype(jnp.bfloat16)
        low = jnp.where(iota((META, total), 0) == col_expert + META // 2, 1.0, 0.0).astype(jnp.bfloat16)
        g_high = dot(meta, high)
        g_low = dot(meta, low)
        below = jnp.where(same & (iota((n, n), 1) <= iota((n, n), 0)), 1.0, 0.0).astype(jnp.bfloat16)
        count = dot(below, jnp.where(g_high > 0.0, 1.0, 0.0).astype(jnp.bfloat16))
        place = lax.rem(iota((n, total), 1), MOST)
        source = lax.rem(iota((n, total), 1), share) // MOST
        good = (g_high > 0.0) & (count == (place + 1).astype(jnp.float32)) & (iota((n, total), 0) // rows == source)
        w_high[w] = jnp.where(good, g_high, 0.0).astype(jnp.bfloat16)
        w_low[w] = jnp.where(good, g_low, 0.0).astype(jnp.bfloat16)

    def gate_up(w):
        if w == 0:
            loads[0].wait()
            loads[1].wait()
        for r in range(1, NEAR):
            b[w, r].wait_recv()
        mine = pl.ds(pl.multiple_of(y * piece, piece), piece)
        tile = 256 if fh % 256 == 0 else 128

        for which, mat in enumerate((wg, wu)):

            @pl.loop(0, fh // tile)
            def _(j, which=which, mat=mat):
                cols = pl.ds(pl.multiple_of(j * tile, tile), tile)
                into = pl.ds(pl.multiple_of(which * fh + j * tile, tile), tile)
                value = dot(incoming[w], mat[:, cols])
                temp[:, 0:tile] = value
                part[w, :, into] = value.astype(jnp.bfloat16)
                own[w, :, into] = temp[mine, 0:tile]

        for r in range(1, reps):
            theirs = pl.ds(pl.multiple_of(lax.rem(y + r, reps) * piece, piece), piece)
            yy[w, r] = copy(part.at[w, theirs], arrived.at[w, r - 1], y_s.at[w, r - 1], y_r.at[w, r - 1], rep_dev(r))
            yy[w, r].start()

    def act(w):
        for r in range(1, reps):
            yy[w, r].wait_recv()
        mine = pl.ds(pl.multiple_of(y * piece, piece), piece)
        tile = 256 if fh % 256 == 0 else 128

        @pl.loop(0, fh // tile)
        def _(j):
            cols = pl.ds(pl.multiple_of(j * tile, tile), tile)
            more = pl.ds(pl.multiple_of(fh + j * tile, tile), tile)
            gate = own[w, :, cols]
            up = own[w, :, more]
            for r in range(reps - 1):
                gate = gate + arrived[w, r, :, cols].astype(jnp.float32)
                up = up + arrived[w, r, :, more].astype(jnp.float32)
            hidden[w, mine, cols] = (gate / (1.0 + jnp.exp(-gate)) * up).astype(jnp.bfloat16)

        for r in range(1, reps):
            hh[w, r] = copy(hidden.at[w, mine], hidden.at[w, mine], h_s.at[w, r - 1], h_r.at[w, r - 1], rep_dev(r))
            hh[w, r].start()

    def down(w):
        if w == 0:
            loads[2].wait()
        for r in range(1, reps):
            hh[w, r].wait_recv()
        tile = 256 if width % 256 == 0 else 128

        @pl.loop(0, width // tile)
        def _(j):
            cols = pl.ds(pl.multiple_of(j * tile, tile), tile)
            out = dot(hidden[w], wd[:, cols]).astype(jnp.bfloat16)
            expert_out[w, :, cols] = out
            returned[w, 0:share, cols] = out[0:share]

        for r in range(1, NEAR):
            span = pl.ds(r * share, share)
            c[w, r] = copy(expert_out.at[w, span], returned.at[w, span], c_s.at[w, r - 1], c_r.at[w, r - 1], near_dev(NEAR - r))
            c[w, r].start()

    def mix(w):
        step, half = divmod(w, halves)
        for r in range(1, NEAR):
            c[w, r].wait_recv()
        tile = 256 if width % 256 == 0 else 128

        @pl.loop(0, width // tile)
        def _(j):
            cols = pl.ds(pl.multiple_of(j * tile, tile), tile)
            value = dot(w_high[w], returned[w, :, cols]) + dot(w_low[w], returned[w, :, cols])
            mixed[w, :, cols] = value.astype(jnp.bfloat16)
            if half == 0:
                kept[step, :, cols] = value[0:rows]

        for k in range(half * src_count, (half + 1) * src_count):
            if k:
                d[step, k] = copy(
                    mixed.at[w, pl.ds((k - half * src_count) * rows, rows)],
                    gathered.at[step, k - 1],
                    d_s.at[step, k - 1],
                    d_r.at[step, k - 1],
                    far_dev(-order[k]),
                )
                d[step, k].start()

    def finish(step):
        for k in range(1, far):
            d[step, k].wait_recv()
        tile = 256 if width % 256 == 0 else 128

        @pl.loop(0, width // tile)
        def _(j):
            cols = pl.ds(pl.multiple_of(j * tile, tile), tile)
            value = kept[step, :, cols]
            for k in range(far - 1):
                value = value + gathered[step, k, :, cols].astype(jnp.float32)
            outs[step][:, cols] = value.astype(jnp.bfloat16)

    stages = {"S": select, "G": gate_up, "A": act, "D": down, "M": mix, "F": finish}
    for name in ORDER:
        stages[name[0]](int(name[1:]))
    for table in (a, b, yy, hh, c, d):
        for item in table.values():
            item.wait_send()


def shards(
    tokens_one,
    tokens_two,
    routes_one,
    routes_two,
    gates_one,
    gates_two,
    place_before,
    swap_flags,
    gate_weight,
    up_weight,
    down_weight,
):
    ep_count = lax.axis_size("ep")
    reps = lax.axis_size("rep")
    half_count = ep_count // 2
    rows, width = tokens_one.shape
    fh = gate_weight.shape[2]
    far = ep_count // NEAR
    indices = jnp.arange(ep_count, dtype=jnp.int32)
    slots_one = jnp.sum(jnp.where(routes_one[:, :, None] == indices, place_before, 0), axis=2)
    partner = jnp.where(indices < half_count, indices + half_count, indices - half_count)
    flagged = jnp.concatenate([swap_flags, swap_flags]) == 1
    source_two = jnp.where(flagged, partner, indices)
    slots_two = jnp.sum(jnp.where(routes_two[:, :, None] == indices, source_two, 0), axis=2)

    def with_meta(tokens, slots, gates):
        lanes = jnp.arange(META, dtype=jnp.int32)
        gate = jnp.sum(jnp.where(slots[:, :, None] == lanes % (META // 2), gates[:, :, None], 0.0), axis=1)
        high = lax.reduce_precision(gate, 8, 7)
        meta = jnp.where(lanes < META // 2, high, gate - high).astype(jnp.bfloat16)
        return jnp.concatenate([tokens, meta], axis=1)

    tok_one = with_meta(tokens_one, slots_one, gates_one)
    tok_two = with_meta(tokens_two, slots_two, gates_two)

    waves = 2 * HALVES
    src_count = far // HALVES
    n = src_count * rows
    total = NEAR * src_count * MOST
    piece = total // reps
    bf16, f32 = jnp.bfloat16, jnp.float32
    dma = pltpu.SemaphoreType.DMA
    vmem = pl.BlockSpec(memory_space=pltpu.VMEM)
    hbm = pl.BlockSpec(memory_space=pl.ANY)
    return pl.pallas_call(
        kernel,
        out_shape=(jax.ShapeDtypeStruct((rows, width), bf16), jax.ShapeDtypeStruct((rows, width), bf16)),
        in_specs=[vmem, vmem, hbm, hbm, hbm],
        out_specs=(vmem, vmem),
        scratch_shapes=[
            pltpu.VMEM((2, far * rows, width + META), bf16),
            pltpu.VMEM((waves, total, width), bf16),
            pltpu.VMEM((waves, total, width), bf16),
            pltpu.VMEM((waves, total, 2 * fh), bf16),
            pltpu.VMEM((waves, piece, 2 * fh), f32),
            pltpu.VMEM((total, 256), f32),
            pltpu.VMEM((waves, reps - 1, piece, 2 * fh), bf16),
            pltpu.VMEM((waves, total, fh), bf16),
            pltpu.VMEM((waves, total, width), bf16),
            pltpu.VMEM((waves, total, width), bf16),
            pltpu.VMEM((waves, n, total), bf16),
            pltpu.VMEM((waves, n, total), bf16),
            pltpu.VMEM((waves, n, width), bf16),
            pltpu.VMEM((2, far - 1, rows, width), bf16),
            pltpu.VMEM((2, rows, width), f32),
            pltpu.VMEM((width, fh), bf16),
            pltpu.VMEM((width, fh), bf16),
            pltpu.VMEM((fh, width), bf16),
            dma((3,)),
            dma((2, far - 1)),
            dma((2, far - 1)),
            dma((waves, NEAR - 1)),
            dma((waves, NEAR - 1)),
            dma((waves, reps - 1)),
            dma((waves, reps - 1)),
            dma((waves, reps - 1)),
            dma((waves, reps - 1)),
            dma((waves, NEAR - 1)),
            dma((waves, NEAR - 1)),
            dma((2, far - 1)),
            dma((2, far - 1)),
        ],
        compiler_params=pltpu.CompilerParams(collective_id=0, has_side_effects=True, vmem_limit_bytes=60 << 20),
    )(tok_one, tok_two, gate_weight[0], up_weight[0], down_weight[0])


def solution(mesh):
    return jax.shard_map(
        shards,
        mesh=mesh,
        in_specs=(
            P("ep", "rep"),
            P("ep", "rep"),
            P("ep", None),
            P("ep", None),
            P("ep", None),
            P("ep", None),
            P(),
            P(),
            P("ep", "rep", None),
            P("ep", "rep", None),
            P("ep", None, "rep"),
        ),
        out_specs=(P("ep", "rep"), P("ep", "rep")),
        check_vma=False,
    )
```

```python
import functools

import jax
import jax.numpy as jnp
from jax import lax
from jax.experimental import pallas as pl
from jax.experimental.pallas import tpu as pltpu
from jax.sharding import PartitionSpec as P

NEAR = 8
MOST = 8
META = 128
FAR_ORDER = (0, 1, 7, 2, 6, 3, 5, 4)
WAVES = (
    (0, 0, 2), (0, 2, 2), (0, 4, 2), (0, 6, 2),
    (1, 2, 2), (1, 4, 2), (1, 6, 2), (1, 0, 2),
)
ORDER = (
    "H01", "H11", "S1", "S4", "H02", "G1", "H03", "S2", "S7", "H12", "G4", "G2", "S3", "A4",
    "A1", "H13", "S5", "S6", "G3", "G7", "S0", "D1", "D4", "A3", "G6", "A2", "G5", "D3",
    "M1", "M4", "A6", "A7", "D2", "M3", "G0", "M2", "D6", "A5", "D7", "A0", "M6", "D5",
    "D0", "M7", "M5", "M0", "F1", "F0",
)
MESH = pl.DeviceIdType.MESH


def dot(a, b):
    return jnp.dot(a, b, preferred_element_type=jnp.float32)


def dot_nt(a, b):
    return lax.dot_general(a, b, (((1,), (1,)), ((), ())), preferred_element_type=jnp.float32)


def iota(shape, dim):
    return lax.broadcasted_iota(jnp.int32, shape, dim)


def kernel(
    tok_one, tok_two, routes_one, routes_two, gates_one, gates_two, table, wg_hbm, wu_hbm, wd_hbm,
    out_one, out_two,
    held, outgo, incoming, part, own, temp, arrived, hidden, expert_out, returned, w_high, w_low, mixed, gathered, kept,
    wg, wu, wd,
    w_sem, a_s, a_r, b_s, b_r, y_s, y_r, h_s, h_r, c_s, c_r, d_s, d_r,
):
    rows, width = tok_one.shape
    padded = width + META
    fh = wg.shape[1]
    far = len(FAR_ORDER)
    reps = arrived[0].shape[0] + 1
    tile = 256
    slot_of = {r: k for k, r in enumerate(FAR_ORDER)}

    ep = lax.axis_index("ep")
    y = lax.axis_index("rep")
    z = ep // NEAR
    near = lax.rem(ep, NEAR)

    def near_dev(r):
        return (z * NEAR + lax.rem(near + r, NEAR), y)

    def far_dev(r):
        return (lax.rem(z + r + far, far) * NEAR + near, y)

    def rep_dev(r):
        return (ep, lax.rem(y + r, reps))

    def copy(src, dst, send, recv, device):
        return pltpu.make_async_remote_copy(
            src_ref=src, dst_ref=dst, send_sem=send, recv_sem=recv, device_id=device, device_id_type=MESH
        )

    outs = (out_one, out_two)
    a, b, yy, hh, c, d = {}, {}, {}, {}, {}, {}

    first = [
        pltpu.make_async_copy(tok, held.at[step, pl.ds(0, rows), pl.ds(0, width)], w_sem.at[3 + step])
        for step, tok in enumerate((tok_one, tok_two))
    ]
    loads = [
        pltpu.make_async_copy(src, dst, w_sem.at[i])
        for i, (src, dst) in enumerate(((wg_hbm, wg), (wu_hbm, wu), (wd_hbm, wd)))
    ]
    for load in first + loads:
        load.start()

    barrier = pltpu.get_barrier_semaphore()
    partners = [near_dev(r) for r in range(1, NEAR)] + [far_dev(r) for r in range(1, far)]
    partners = partners + [rep_dev(r) for r in range(1, reps)]
    for device in partners:
        pl.semaphore_signal(barrier, inc=1, device_id=device, device_id_type=MESH)

    experts = META // 2
    for step, (routes, gates) in enumerate(((routes_one, gates_one), (routes_two, gates_two))):
        lanes = iota((experts, rows), 0)
        value = jnp.zeros((experts, rows), jnp.float32)
        for k in range(routes.shape[0]):
            value = value + jnp.where(lanes == routes[k : k + 1, :], gates[k : k + 1, :], 0.0)
        high = value.astype(jnp.bfloat16)
        low = (value - high.astype(jnp.float32)).astype(jnp.bfloat16)
        eye = jnp.where(iota((rows, rows), 0) == iota((rows, rows), 1), 1.0, 0.0).astype(jnp.bfloat16)
        high = dot_nt(eye, high).astype(jnp.bfloat16)
        low = dot_nt(eye, low).astype(jnp.bfloat16)
        slot = table[step : step + 1, 0:experts]
        line = iota((META, experts), 0)
        to_high = jnp.where(slot == line, 1.0, 0.0).astype(jnp.bfloat16)
        to_low = jnp.where(slot + experts == line, 1.0, 0.0).astype(jnp.bfloat16)
        meta = dot_nt(high, to_high) + dot_nt(low, to_low)
        held[step, 0:rows, width:padded] = meta.astype(jnp.bfloat16)
    for load in first:
        load.wait()
    pl.semaphore_wait(barrier, len(partners))

    def block(step, r, cut=None):
        at = slot_of[r] * rows
        if cut is None:
            return held.at[step, pl.ds(at, rows)]
        return held.at[step, pl.ds(at + cut * (rows // 2), rows // 2)]

    def hop(step, h):
        cuts = (0, 1) if 2 * h == far else (None, None)
        for way, sign in enumerate((1, -1)):
            src = block(step, (sign * (h - 1)) % far, cuts[way])
            dst = block(step, (sign * h) % far, cuts[way])
            i = 2 * (h - 1) + way
            a[step, h, way] = copy(src, dst, a_s.at[step, i], a_r.at[step, i], far_dev(sign))
            a[step, h, way].start()

    seen = set()

    def landed(step, h):
        if (step, h) not in seen:
            seen.add((step, h))
            for way in range(2):
                a[step, h, way].wait_recv()

    def relay(code):
        step, h = divmod(code, 10)
        landed(step, h)
        hop(step, h + 1)

    def shape_of(w):
        step, base, count = WAVES[w]
        share = count * MOST
        return step, base, count, count * rows, share, NEAR * share, NEAR * share // reps

    def select(w):
        step, base, count, n, share, total, piece = shape_of(w)
        for r in sorted(FAR_ORDER[base : base + count]):
            if r:
                landed(step, min(r, far - r))
        at = base * rows
        meta = held[step, at : at + n, width:padded]
        row_expert = z * NEAR + lax.rem(near + iota((total, META), 0) // share, NEAR)
        pick = jnp.where(iota((total, META), 1) == row_expert, 1.0, 0.0).astype(jnp.bfloat16)
        value = dot_nt(pick, meta)
        same = iota((n, n), 0) // rows == iota((n, n), 1) // rows
        upto = jnp.where(same & (iota((n, n), 0) <= iota((n, n), 1)), 1.0, 0.0).astype(jnp.bfloat16)
        number = dot(jnp.where(value > 0.0, 1.0, 0.0).astype(jnp.bfloat16), upto)
        place = lax.rem(iota((total, n), 0), MOST)
        source = lax.rem(iota((total, n), 0), share) // MOST
        good = (value > 0.0) & (number == (place + 1).astype(jnp.float32)) & (iota((total, n), 1) // rows == source)
        chosen = jnp.where(good, 1.0, 0.0).astype(jnp.bfloat16)

        @pl.loop(0, width // tile)
        def _(j):
            cols = pl.ds(pl.multiple_of(j * tile, tile), tile)
            out = dot(chosen, held[step, at : at + n, cols]).astype(jnp.bfloat16)
            outgo[w][:, cols] = out
            incoming[w][0:share, cols] = out[0:share]

        for r in range(1, NEAR):
            span = pl.ds(r * share, share)
            b[w, r] = copy(outgo[w].at[span], incoming[w].at[span], b_s.at[w, r - 1], b_r.at[w, r - 1], near_dev(r))
            b[w, r].start()

    def weigh(w):
        step, base, count, n, share, total, piece = shape_of(w)
        at = base * rows
        meta = held[step, at : at + n, width:padded]
        same = iota((n, n), 0) // rows == iota((n, n), 1) // rows
        col_expert = z * NEAR + lax.rem(near + iota((META, total), 1) // share, NEAR)
        high = jnp.where(iota((META, total), 0) == col_expert, 1.0, 0.0).astype(jnp.bfloat16)
        low = jnp.where(iota((META, total), 0) == col_expert + META // 2, 1.0, 0.0).astype(jnp.bfloat16)
        g_high = dot(meta, high)
        g_low = dot(meta, low)
        below = jnp.where(same & (iota((n, n), 1) <= iota((n, n), 0)), 1.0, 0.0).astype(jnp.bfloat16)
        number = dot(below, jnp.where(g_high > 0.0, 1.0, 0.0).astype(jnp.bfloat16))
        place = lax.rem(iota((n, total), 1), MOST)
        source = lax.rem(iota((n, total), 1), share) // MOST
        good = (g_high > 0.0) & (number == (place + 1).astype(jnp.float32)) & (iota((n, total), 0) // rows == source)
        w_high[w][...] = jnp.where(good, g_high, 0.0).astype(jnp.bfloat16)
        w_low[w][...] = jnp.where(good, g_low, 0.0).astype(jnp.bfloat16)

    loaded = set()

    def need(i):
        if i not in loaded:
            loads[i].wait()
            loaded.add(i)

    def gate_up(w):
        step, base, count, n, share, total, piece = shape_of(w)
        need(0)
        need(1)
        for r in range(1, NEAR):
            b[w, r].wait_recv()
        mine = pl.ds(pl.multiple_of(y * piece, piece), piece)

        for which, mat in enumerate((wg, wu)):

            @pl.loop(0, fh // tile)
            def _(j, which=which, mat=mat):
                cols = pl.ds(pl.multiple_of(j * tile, tile), tile)
                into = pl.ds(pl.multiple_of(which * fh + j * tile, tile), tile)
                value = dot(incoming[w][...], mat[:, cols])
                temp[0:total, :] = value
                part[w][:, into] = value.astype(jnp.bfloat16)
                own[w][:, into] = temp[mine, :]

        for r in range(1, reps):
            theirs = pl.ds(pl.multiple_of(lax.rem(y + r, reps) * piece, piece), piece)
            yy[w, r] = copy(part[w].at[theirs], arrived[w].at[r - 1], y_s.at[w, r - 1], y_r.at[w, r - 1], rep_dev(r))
            yy[w, r].start()
        weigh(w)

    def act(w):
        step, base, count, n, share, total, piece = shape_of(w)
        for r in range(1, reps):
            yy[w, r].wait_recv()
        mine = pl.ds(pl.multiple_of(y * piece, piece), piece)

        @pl.loop(0, fh // tile)
        def _(j):
            cols = pl.ds(pl.multiple_of(j * tile, tile), tile)
            more = pl.ds(pl.multiple_of(fh + j * tile, tile), tile)
            gate = own[w][:, cols]
            up = own[w][:, more]
            for r in range(reps - 1):
                gate = gate + arrived[w][r, :, cols].astype(jnp.float32)
                up = up + arrived[w][r, :, more].astype(jnp.float32)
            hidden[w][mine, cols] = (gate / (1.0 + jnp.exp(-gate)) * up).astype(jnp.bfloat16)

        for r in range(1, reps):
            hh[w, r] = copy(
                hidden[w].at[mine], hidden[w].at[mine], h_s.at[w, r - 1], h_r.at[w, r - 1], rep_dev(r)
            )
            hh[w, r].start()

    def down(w):
        step, base, count, n, share, total, piece = shape_of(w)
        need(2)
        for r in range(1, reps):
            hh[w, r].wait_recv()

        @pl.loop(0, width // tile)
        def _(j):
            cols = pl.ds(pl.multiple_of(j * tile, tile), tile)
            out = dot(hidden[w][...], wd[:, cols]).astype(jnp.bfloat16)
            expert_out[w][:, cols] = out
            returned[w][0:share, cols] = out[0:share]

        for r in range(1, NEAR):
            span = pl.ds(r * share, share)
            c[w, r] = copy(
                expert_out[w].at[span], returned[w].at[span], c_s.at[w, r - 1], c_r.at[w, r - 1], near_dev(NEAR - r)
            )
            c[w, r].start()

    def mix(w):
        step, base, count, n, share, total, piece = shape_of(w)
        for r in range(1, NEAR):
            c[w, r].wait_recv()

        @pl.loop(0, width // tile)
        def _(j):
            cols = pl.ds(pl.multiple_of(j * tile, tile), tile)
            value = dot(w_high[w][...], returned[w][:, cols]) + dot(w_low[w][...], returned[w][:, cols])
            mixed[w][:, cols] = value.astype(jnp.bfloat16)
            if base == 0:
                kept[step, :, cols] = value[0:rows]

        for k in range(max(base, 1), base + count):
            d[step, k] = copy(
                mixed[w].at[pl.ds((k - base) * rows, rows)],
                gathered.at[step, k - 1],
                d_s.at[step, k - 1],
                d_r.at[step, k - 1],
                far_dev(-FAR_ORDER[k]),
            )
            d[step, k].start()

    def finish(step):
        for k in range(1, far):
            d[step, k].wait_recv()

        @pl.loop(0, width // tile)
        def _(j):
            cols = pl.ds(pl.multiple_of(j * tile, tile), tile)
            value = kept[step, :, cols]
            for k in range(far - 1):
                value = value + gathered[step, k, :, cols].astype(jnp.float32)
            outs[step][:, cols] = value.astype(jnp.bfloat16)

    hop(0, 1)
    hop(1, 1)
    stages = {"H": relay, "S": select, "G": gate_up, "A": act, "D": down, "M": mix, "F": finish}
    for name in ORDER:
        stages[name[0]](int(name[1:]))
    for copies in (a, b, yy, hh, c, d):
        for item in copies.values():
            item.wait_send()


def shards(
    tokens_one,
    tokens_two,
    routes_one,
    routes_two,
    gates_one,
    gates_two,
    place_before,
    swap_flags,
    gate_weight,
    up_weight,
    down_weight,
):
    ep_count = lax.axis_size("ep")
    reps = lax.axis_size("rep")
    half_count = ep_count // 2
    rows, width = tokens_one.shape
    fh = gate_weight.shape[2]
    far = ep_count // NEAR
    indices = jnp.arange(ep_count, dtype=jnp.int32)
    partner = jnp.where(indices < half_count, indices + half_count, indices - half_count)
    flagged = jnp.concatenate([swap_flags, swap_flags]) == 1
    source_two = jnp.where(flagged, partner, indices)
    table = jnp.stack([place_before, source_two])

    sizes = []
    for step, base, count in WAVES:
        total = NEAR * count * MOST
        sizes.append((count * rows, total, total // reps))
    waves = len(WAVES)
    bf16, f32 = jnp.bfloat16, jnp.float32
    dma = pltpu.SemaphoreType.DMA
    vmem = pl.BlockSpec(memory_space=pltpu.VMEM)
    hbm = pl.BlockSpec(memory_space=pl.ANY)
    return pl.pallas_call(
        kernel,
        out_shape=(jax.ShapeDtypeStruct((rows, width), bf16), jax.ShapeDtypeStruct((rows, width), bf16)),
        in_specs=[hbm, hbm, vmem, vmem, vmem, vmem, vmem, hbm, hbm, hbm],
        out_specs=(vmem, vmem),
        scratch_shapes=[
            pltpu.VMEM((2, far * rows, width + META), bf16),
            [pltpu.VMEM((total, width), bf16) for n, total, piece in sizes],
            [pltpu.VMEM((total, width), bf16) for n, total, piece in sizes],
            [pltpu.VMEM((total, 2 * fh), bf16) for n, total, piece in sizes],
            [pltpu.VMEM((piece, 2 * fh), f32) for n, total, piece in sizes],
            pltpu.VMEM((max(total for n, total, piece in sizes), 256), f32),
            [pltpu.VMEM((reps - 1, piece, 2 * fh), bf16) for n, total, piece in sizes],
            [pltpu.VMEM((total, fh), bf16) for n, total, piece in sizes],
            [pltpu.VMEM((total, width), bf16) for n, total, piece in sizes],
            [pltpu.VMEM((total, width), bf16) for n, total, piece in sizes],
            [pltpu.VMEM((n, total), bf16) for n, total, piece in sizes],
            [pltpu.VMEM((n, total), bf16) for n, total, piece in sizes],
            [pltpu.VMEM((n, width), bf16) for n, total, piece in sizes],
            pltpu.VMEM((2, far - 1, rows, width), bf16),
            pltpu.VMEM((2, rows, width), f32),
            pltpu.VMEM((width, fh), bf16),
            pltpu.VMEM((width, fh), bf16),
            pltpu.VMEM((fh, width), bf16),
            dma((5,)),
            dma((2, far)),
            dma((2, far)),
            dma((waves, NEAR - 1)),
            dma((waves, NEAR - 1)),
            dma((waves, reps - 1)),
            dma((waves, reps - 1)),
            dma((waves, reps - 1)),
            dma((waves, reps - 1)),
            dma((waves, NEAR - 1)),
            dma((waves, NEAR - 1)),
            dma((2, far - 1)),
            dma((2, far - 1)),
        ],
        compiler_params=pltpu.CompilerParams(collective_id=0, has_side_effects=True, vmem_limit_bytes=62 << 20),
    )(
        tokens_one, tokens_two, routes_one.T, routes_two.T, gates_one.T, gates_two.T, table,
        gate_weight[0], up_weight[0], down_weight[0],
    )


def solution(mesh):
    return jax.shard_map(
        shards,
        mesh=mesh,
        in_specs=(
            P("ep", "rep"),
            P("ep", "rep"),
            P("ep", None),
            P("ep", None),
            P("ep", None),
            P("ep", None),
            P(),
            P(),
            P("ep", "rep", None),
            P("ep", "rep", None),
            P("ep", None, "rep"),
        ),
        out_specs=(P("ep", "rep"), P("ep", "rep")),
        check_vma=False,
    )
```

```python
import functools

import jax
import jax.numpy as jnp
from jax import lax
from jax.experimental import pallas as pl
from jax.experimental.pallas import tpu as pltpu
from jax.sharding import PartitionSpec as P

NEAR = 8
MOST = 8
META = 128
FAR_ORDER = (0, 1, 7, 2, 6, 3, 5, 4)
WAVES = (
    (0, 0, 2), (0, 2, 2), (0, 4, 2), (0, 6, 2),
    (1, 2, 2), (1, 4, 2), (1, 6, 2), (1, 0, 2),
)
ORDER = (
    "H01", "S0", "H02", "S1", "H11", "G0", "S2", "H03", "H12", "G1", "S3", "R0", "S5", "R1",
    "G2", "S7", "A1", "H13", "A0", "G3", "S4", "R2", "R3", "X0", "X1", "S6", "A2", "A3",
    "G5", "D1", "X3", "X2", "G7", "G4", "D3", "R5", "G6", "M1", "D2", "A5", "R6", "M3",
    "R4", "D0", "X5", "A6", "M2", "R7", "D5", "X6", "A4", "X4", "D6", "A7", "M0", "M5",
    "X7", "D4", "M6", "D7", "M4", "M7", "F0", "F1",
)
MESH = pl.DeviceIdType.MESH


def dot(a, b):
    return jnp.dot(a, b, preferred_element_type=jnp.float32)


def dot_nt(a, b):
    return lax.dot_general(a, b, (((1,), (1,)), ((), ())), preferred_element_type=jnp.float32)


def iota(shape, dim):
    return lax.broadcasted_iota(jnp.int32, shape, dim)


def kernel(
    tok_one, tok_two, routes_one, routes_two, gates_one, gates_two, place, flags, wg_hbm, wu_hbm, wd_hbm,
    out,
    held, outgo, incoming, part, own, next_own, temp, far_part, arrived, hidden, expert_out, returned, w_high, w_low, mixed, gathered, kept,
    wg, wu, wd,
    w_sem, a_s, a_r, b_s, b_r, y_s, y_r, h_s, h_r, c_s, c_r, d_s, d_r,
):
    rows, width = tok_one.shape
    padded = width + META
    fh = wg.shape[1]
    far = len(FAR_ORDER)
    reps = 4
    tile = fh // 2
    wide = width // 2
    slot_of = {r: k for k, r in enumerate(FAR_ORDER)}

    ep = lax.axis_index("ep")
    y = lax.axis_index("rep")
    z = ep // NEAR
    near = lax.rem(ep, NEAR)

    def near_dev(r):
        return (z * NEAR + lax.rem(near + r, NEAR), y)

    def far_dev(r):
        return (lax.rem(z + r + far, far) * NEAR + near, y)

    def rep_dev(r):
        return (ep, lax.rem(y + r, reps))

    def copy(src, dst, send, recv, device):
        return pltpu.make_async_remote_copy(
            src_ref=src, dst_ref=dst, send_sem=send, recv_sem=recv, device_id=device, device_id_type=MESH
        )

    a, b, yy, hh, c, d = {}, {}, {}, {}, {}, {}

    first = [
        pltpu.make_async_copy(tok, held.at[step, pl.ds(0, rows), pl.ds(0, width)], w_sem.at[3 + step])
        for step, tok in enumerate((tok_one, tok_two))
    ]
    loads = [
        pltpu.make_async_copy(src, dst, w_sem.at[i])
        for i, (src, dst) in enumerate(((wg_hbm, wg), (wu_hbm, wu), (wd_hbm, wd)))
    ]
    for load in first + loads:
        load.start()

    barrier = pltpu.get_barrier_semaphore()
    partners = [near_dev(r) for r in range(1, NEAR)] + [far_dev(r) for r in range(1, far)]
    partners = partners + [rep_dev(r) for r in range(1, reps)]
    for device in partners:
        pl.semaphore_signal(barrier, inc=1, device_id=device, device_id_type=MESH)

    experts = META // 2
    half = experts // 2
    lane = iota((1, experts), 1)
    twice = jnp.where(iota((half, experts), 0) == lax.rem(iota((half, experts), 1), half), 1.0, 0.0)
    flagged = jnp.broadcast_to(flags[...].astype(jnp.float32), (8, half))
    flagged = dot(flagged.astype(jnp.bfloat16), twice.astype(jnp.bfloat16))[0:1, :]
    moved = jnp.where(flagged > 0.5, jnp.where(lane < half, lane + half, lane - half), lane)
    slots = (place[...], moved)
    for step, (routes, gates) in enumerate(((routes_one, gates_one), (routes_two, gates_two))):
        lanes = iota((experts, rows), 0)
        value = jnp.zeros((experts, rows), jnp.float32)
        for k in range(routes.shape[0]):
            value = value + jnp.where(lanes == routes[k : k + 1, :], gates[k : k + 1, :], 0.0)
        high = value.astype(jnp.bfloat16)
        low = (value - high.astype(jnp.float32)).astype(jnp.bfloat16)
        eye = jnp.where(iota((rows, rows), 0) == iota((rows, rows), 1), 1.0, 0.0).astype(jnp.bfloat16)
        high = dot_nt(eye, high).astype(jnp.bfloat16)
        low = dot_nt(eye, low).astype(jnp.bfloat16)
        slot = slots[step]
        line = iota((META, experts), 0)
        to_high = jnp.where(slot == line, 1.0, 0.0).astype(jnp.bfloat16)
        to_low = jnp.where(slot + experts == line, 1.0, 0.0).astype(jnp.bfloat16)
        meta = dot_nt(high, to_high) + dot_nt(low, to_low)
        held[step, 0:rows, width:padded] = meta.astype(jnp.bfloat16)
    for load in first:
        load.wait()
    pl.semaphore_wait(barrier, len(partners))

    def block(step, r, cut=None):
        at = slot_of[r] * rows
        if cut is None:
            return held.at[step, pl.ds(at, rows)]
        return held.at[step, pl.ds(at + cut * (rows // 2), rows // 2)]

    def hop(step, h):
        cuts = (0, 1) if 2 * h == far else (None, None)
        for way, sign in enumerate((1, -1)):
            src = block(step, (sign * (h - 1)) % far, cuts[way])
            dst = block(step, (sign * h) % far, cuts[way])
            i = 2 * (h - 1) + way
            a[step, h, way] = copy(src, dst, a_s.at[step, i], a_r.at[step, i], far_dev(sign))
            a[step, h, way].start()

    seen = set()

    def landed(step, h):
        if (step, h) not in seen:
            seen.add((step, h))
            for way in range(2):
                a[step, h, way].wait_recv()

    def relay(code):
        step, h = divmod(code, 10)
        landed(step, h)
        hop(step, h + 1)

    def shape_of(w):
        step, base, count = WAVES[w]
        share = count * MOST
        return step, base, count, count * rows, share, NEAR * share, NEAR * share // reps

    def select(w):
        step, base, count, n, share, total, piece = shape_of(w)
        for r in sorted(FAR_ORDER[base : base + count]):
            if r:
                landed(step, min(r, far - r))
        at = base * rows
        meta = held[step, at : at + n, width:padded]
        row_expert = z * NEAR + lax.rem(near + iota((total, META), 0) // share, NEAR)
        pick = jnp.where(iota((total, META), 1) == row_expert, 1.0, 0.0).astype(jnp.bfloat16)
        value = dot_nt(pick, meta)
        same = iota((n, n), 0) // rows == iota((n, n), 1) // rows
        upto = jnp.where(same & (iota((n, n), 0) <= iota((n, n), 1)), 1.0, 0.0).astype(jnp.bfloat16)
        number = dot(jnp.where(value > 0.0, 1.0, 0.0).astype(jnp.bfloat16), upto)
        place = lax.rem(iota((total, n), 0), MOST)
        source = lax.rem(iota((total, n), 0), share) // MOST
        good = (value > 0.0) & (number == (place + 1).astype(jnp.float32)) & (iota((total, n), 1) // rows == source)
        chosen = jnp.where(good, 1.0, 0.0).astype(jnp.bfloat16)

        @pl.loop(0, width // wide)
        def _(j):
            cols = pl.ds(pl.multiple_of(j * wide, 128), wide)
            out = dot(chosen, held[step, at : at + n, cols]).astype(jnp.bfloat16)
            outgo[w][:, cols] = out
            incoming[w][0:share, cols] = out[0:share]

        for r in range(1, NEAR):
            span = pl.ds(r * share, share)
            b[w, r] = copy(outgo[w].at[span], incoming[w].at[span], b_s.at[w, r - 1], b_r.at[w, r - 1], near_dev(r))
            b[w, r].start()

    def weigh(w):
        step, base, count, n, share, total, piece = shape_of(w)
        at = base * rows
        meta = held[step, at : at + n, width:padded]
        same = iota((n, n), 0) // rows == iota((n, n), 1) // rows
        col_expert = z * NEAR + lax.rem(near + iota((META, total), 1) // share, NEAR)
        high = jnp.where(iota((META, total), 0) == col_expert, 1.0, 0.0).astype(jnp.bfloat16)
        low = jnp.where(iota((META, total), 0) == col_expert + META // 2, 1.0, 0.0).astype(jnp.bfloat16)
        g_high = dot(meta, high)
        g_low = dot(meta, low)
        below = jnp.where(same & (iota((n, n), 1) <= iota((n, n), 0)), 1.0, 0.0).astype(jnp.bfloat16)
        number = dot(below, jnp.where(g_high > 0.0, 1.0, 0.0).astype(jnp.bfloat16))
        place = lax.rem(iota((n, total), 1), MOST)
        source = lax.rem(iota((n, total), 1), share) // MOST
        good = (g_high > 0.0) & (number == (place + 1).astype(jnp.float32)) & (iota((n, total), 0) // rows == source)
        w_high[w][...] = jnp.where(good, g_high, 0.0).astype(jnp.bfloat16)
        w_low[w][...] = jnp.where(good, g_low, 0.0).astype(jnp.bfloat16)

    loaded = set()

    def need(i):
        if i not in loaded:
            loads[i].wait()
            loaded.add(i)

    def gate_up(w):
        step, base, count, n, share, total, piece = shape_of(w)
        need(0)
        need(1)
        for r in range(1, NEAR):
            b[w, r].wait_recv()
        mine = pl.ds(pl.multiple_of(y * piece, piece), piece)

        for which, mat in enumerate((wg, wu)):

            @pl.loop(0, fh // tile)
            def _(j, which=which, mat=mat):
                cols = pl.ds(pl.multiple_of(j * tile, tile), tile)
                into = pl.ds(pl.multiple_of(which * fh + j * tile, tile), tile)
                value = dot(incoming[w][...], mat[:, cols])
                temp[0:total, :] = value
                part[w][:, into] = value.astype(jnp.bfloat16)
                own[w][:, into] = temp[mine, :]
                next_own[w][:, into] = temp[rows_of(w, (1, reps - 1)[which]), :]

        gates, ups = pl.ds(0, fh), pl.ds(fh, fh)
        across, after, before = rows_of(w, 2), rows_of(w, 1), rows_of(w, reps - 1)
        to_rep(w, 0, part[w].at[across, gates], far_part[w].at[0], 1)
        to_rep(w, 1, part[w].at[across, ups], far_part[w].at[1], reps - 1)
        to_rep(w, 2, part[w].at[after, ups], arrived[w].at[0, :, ups], 1)
        to_rep(w, 3, part[w].at[before, gates], arrived[w].at[1, :, gates], reps - 1)
        weigh(w)

    def rows_of(w, r):
        piece = shape_of(w)[-1]
        return pl.ds(pl.multiple_of(lax.rem(y + r, reps) * piece, piece), piece)

    def to_rep(w, i, src, dst, r):
        yy[w, i] = copy(src, dst, y_s.at[w, i], y_r.at[w, i], rep_dev(r))
        yy[w, i].start()

    def reduce(w):
        gates, ups = pl.ds(0, fh), pl.ds(fh, fh)
        for i, (r, cols) in enumerate(((1, gates), (reps - 1, ups))):
            yy[w, i].wait_recv()
            line = rows_of(w, r)
            value = next_own[w][:, cols] + far_part[w][i].astype(jnp.float32)
            part[w][line, cols] = value.astype(jnp.bfloat16)
            to_rep(w, 4 + i, part[w].at[line, cols], arrived[w].at[i, :, cols], r)

    def act(w):
        step, base, count, n, share, total, piece = shape_of(w)
        for i in range(2, 6):
            yy[w, i].wait_recv()
        mine = pl.ds(pl.multiple_of(y * piece, piece), piece)

        @pl.loop(0, fh // tile)
        def _(j):
            cols = pl.ds(pl.multiple_of(j * tile, tile), tile)
            more = pl.ds(pl.multiple_of(fh + j * tile, tile), tile)
            gate = own[w][:, cols]
            up = own[w][:, more]
            for r in range(2):
                gate = gate + arrived[w][r, :, cols].astype(jnp.float32)
                up = up + arrived[w][r, :, more].astype(jnp.float32)
            hidden[w][mine, cols] = (gate / (1.0 + jnp.exp(-gate)) * up).astype(jnp.bfloat16)

        share_hidden(w, 0, hidden[w].at[mine], 1)
        share_hidden(w, 1, hidden[w].at[mine], reps - 1)

    def share_hidden(w, i, ref, r):
        hh[w, i] = copy(ref, ref, h_s.at[w, i], h_r.at[w, i], rep_dev(r))
        hh[w, i].start()

    def across(w):
        for i, r in enumerate((1, reps - 1)):
            hh[w, i].wait_recv()
            share_hidden(w, 2 + i, hidden[w].at[rows_of(w, reps - r), pl.ds(i * (fh // 2), fh // 2)], r)

    def down(w):
        step, base, count, n, share, total, piece = shape_of(w)
        need(2)
        for i in range(2, 4):
            hh[w, i].wait_recv()

        @pl.loop(0, width // wide)
        def _(j):
            cols = pl.ds(pl.multiple_of(j * wide, 128), wide)
            out = dot(hidden[w][...], wd[:, cols]).astype(jnp.bfloat16)
            expert_out[w][:, cols] = out
            returned[w][0:share, cols] = out[0:share]

        for r in range(1, NEAR):
            span = pl.ds(r * share, share)
            c[w, r] = copy(
                expert_out[w].at[span], returned[w].at[span], c_s.at[w, r - 1], c_r.at[w, r - 1], near_dev(NEAR - r)
            )
            c[w, r].start()

    def mix(w):
        step, base, count, n, share, total, piece = shape_of(w)
        for r in range(1, NEAR):
            c[w, r].wait_recv()

        @pl.loop(0, width // wide)
        def _(j):
            cols = pl.ds(pl.multiple_of(j * wide, 128), wide)
            value = dot(w_high[w][...], returned[w][:, cols]) + dot(w_low[w][...], returned[w][:, cols])
            mixed[w][:, cols] = value.astype(jnp.bfloat16)
            if base == 0:
                kept[step, :, cols] = value[0:rows]

        for k in range(max(base, 1), base + count):
            d[step, k] = copy(
                mixed[w].at[pl.ds((k - base) * rows, rows)],
                gathered.at[step, k - 1],
                d_s.at[step, k - 1],
                d_r.at[step, k - 1],
                far_dev(-FAR_ORDER[k]),
            )
            d[step, k].start()

    def finish(step):
        for k in range(1, far):
            d[step, k].wait_recv()

        @pl.loop(0, width // wide)
        def _(j):
            cols = pl.ds(pl.multiple_of(j * wide, 128), wide)
            value = kept[step, :, cols]
            for k in range(far - 1):
                value = value + gathered[step, k, :, cols].astype(jnp.float32)
            out[step, :, cols] = value.astype(jnp.bfloat16)

    hop(0, 1)
    hop(1, 1)
    stages = {"H": relay, "S": select, "G": gate_up, "R": reduce, "A": act, "X": across, "D": down, "M": mix, "F": finish}
    for name in ORDER:
        stages[name[0]](int(name[1:]))
    for copies in (a, b, yy, hh, c, d):
        for item in copies.values():
            item.wait_send()


def shards(
    tokens_one,
    tokens_two,
    routes_one,
    routes_two,
    gates_one,
    gates_two,
    place_before,
    swap_flags,
    gate_weight,
    up_weight,
    down_weight,
):
    ep_count = lax.axis_size("ep")
    reps = lax.axis_size("rep")
    rows, width = tokens_one.shape
    fh = gate_weight.shape[2]
    far = ep_count // NEAR
    sizes = []
    for step, base, count in WAVES:
        total = NEAR * count * MOST
        sizes.append((count * rows, total, total // reps))
    waves = len(WAVES)
    bf16, f32 = jnp.bfloat16, jnp.float32
    dma = pltpu.SemaphoreType.DMA
    vmem = pl.BlockSpec(memory_space=pltpu.VMEM)
    hbm = pl.BlockSpec(memory_space=pl.ANY)
    mixed = pl.pallas_call(
        kernel,
        out_shape=jax.ShapeDtypeStruct((2, rows, width), bf16),
        in_specs=[hbm, hbm, vmem, vmem, vmem, vmem, vmem, vmem, hbm, hbm, hbm],
        out_specs=vmem,
        scratch_shapes=[
            pltpu.VMEM((2, far * rows, width + META), bf16),
            [pltpu.VMEM((total, width), bf16) for n, total, piece in sizes],
            [pltpu.VMEM((total, width), bf16) for n, total, piece in sizes],
            [pltpu.VMEM((total, 2 * fh), bf16) for n, total, piece in sizes],
            [pltpu.VMEM((piece, 2 * fh), f32) for n, total, piece in sizes],
            [pltpu.VMEM((piece, 2 * fh), f32) for n, total, piece in sizes],
            pltpu.VMEM((max(total for n, total, piece in sizes), fh // 2), f32),
            [pltpu.VMEM((2, piece, fh), bf16) for n, total, piece in sizes],
            [pltpu.VMEM((2, piece, 2 * fh), bf16) for n, total, piece in sizes],
            [pltpu.VMEM((total, fh), bf16) for n, total, piece in sizes],
            [pltpu.VMEM((total, width), bf16) for n, total, piece in sizes],
            [pltpu.VMEM((total, width), bf16) for n, total, piece in sizes],
            [pltpu.VMEM((n, total), bf16) for n, total, piece in sizes],
            [pltpu.VMEM((n, total), bf16) for n, total, piece in sizes],
            [pltpu.VMEM((n, width), bf16) for n, total, piece in sizes],
            pltpu.VMEM((2, far - 1, rows, width), bf16),
            pltpu.VMEM((2, rows, width), f32),
            pltpu.VMEM((width, fh), bf16),
            pltpu.VMEM((width, fh), bf16),
            pltpu.VMEM((fh, width), bf16),
            dma((5,)),
            dma((2, far)),
            dma((2, far)),
            dma((waves, NEAR - 1)),
            dma((waves, NEAR - 1)),
            dma((waves, 6)),
            dma((waves, 6)),
            dma((waves, 4)),
            dma((waves, 4)),
            dma((waves, NEAR - 1)),
            dma((waves, NEAR - 1)),
            dma((2, far - 1)),
            dma((2, far - 1)),
        ],
        compiler_params=pltpu.CompilerParams(collective_id=0, has_side_effects=True, vmem_limit_bytes=62 << 20),
    )(
        tokens_one, tokens_two, routes_one.T, routes_two.T, gates_one.T, gates_two.T,
        place_before[None, :], swap_flags[None, :],
        gate_weight[0], up_weight[0], down_weight[0],
    )
    return mixed[0], mixed[1]


def solution(mesh):
    return jax.shard_map(
        shards,
        mesh=mesh,
        in_specs=(
            P("ep", "rep"),
            P("ep", "rep"),
            P("ep", None),
            P("ep", None),
            P("ep", None),
            P("ep", None),
            P(),
            P(),
            P("ep", "rep", None),
            P("ep", "rep", None),
            P("ep", None, "rep"),
        ),
        out_specs=(P("ep", "rep"), P("ep", "rep")),
        check_vma=False,
    )
```
